128 devices in a mesh: section: 8 (over x, core), space: 16 (over y, z).
Axes of the slice: x: 4, y: 4, z: 4, core: 2. Of those that a mesh axis runs over, the one named last changes fastest.
Arguments:
- features: bfloat16 [8, 2, 256, 1024], P(None, None, 'space'), may hold values from -6 to 6
- lift_w: bfloat16 [2, 32], replicated, may hold values from -4 to 4
- spec_w: bfloat16 [8, 64, 128, 32, 64], P('section', 'space'), may hold values from -3 to 3
- point_w: bfloat16 [8, 32, 32], P('section'), may hold values from -1.5 to 1.5
- point_b: bfloat16 [8, 32], P('section'), may hold values from -3 to 3
Outputs:
- saved: bfloat16 [8, 8, 32, 256, 1024], P('section', None, None, 'space')
The draws below stay inside these ranges and needn't reach their ends.
All inputs are finite; a program needn't handle non-finite values.
Results may differ from the reference program's by a relative error of at most 0.03.
Values may be sent and summed in bfloat16 or wider, within the bound.
A program may use at most 128 MiB of HBM per device.

```python
import jax
import jax.numpy as jnp

CHANNELS = 32
COLS = 1024
MODES_W = 64
MODES_H = 128
FEATURES = 2
MICRO = 8
LAYERS = 8
ROWS = 256


def block_levels(rng, extent, pieces, smallest, high):
    def one(axis_at, parts):
        steps = jax.random.uniform(jax.random.fold_in(jax.random.fold_in(rng, 6), axis_at), (parts,), jnp.float32, smallest / len(pieces), high / len(pieces))
        return jnp.repeat(jnp.exp(steps), extent[axis_at] // parts).reshape((-1,) + (1,) * (len(extent) - axis_at - 1))

    loudness = one(*pieces[0])
    for cut in pieces[1:]:
        loudness = loudness * one(*cut)
    return loudness


def bell_draw(own_key, extent, width, limit, cuts=(), held_as=jnp.bfloat16):
    factor_of = block_levels(own_key, extent, cuts, -0.22, 0.18) if cuts else 1.0
    drawn = jax.random.normal(own_key, extent, jnp.float32) * width * factor_of
    return jnp.minimum(jnp.maximum(drawn, -limit), limit).astype(held_as)


def setup_inputs(seed: int = 0) -> dict:
    splits = jax.random.split(jax.random.key(seed), 6)
    return {
        "features": bell_draw(splits[0], (MICRO, FEATURES, ROWS, COLS), 1.0, 6.0, ((2, 16),)),
        "lift_w": bell_draw(splits[1], (FEATURES, CHANNELS), FEATURES ** -0.5, 4.0),
        "spec_w": bell_draw(splits[2], (LAYERS, MODES_W, MODES_H, CHANNELS, 2 * CHANNELS), 0.2, 3.0, ((0, 8), (1, 16))),
        "point_w": bell_draw(splits[3], (LAYERS, CHANNELS, CHANNELS), (CHANNELS // 2) ** -0.5, 1.5, ((0, 8),)),
        "point_b": bell_draw(splits[4], (LAYERS, CHANNELS), 0.5, 3.0, ((0, 8),)),
    }


def turn_table(first, second, period):
    product = (first[:, None] * second[None, :]) % period
    return 2.0 * jnp.pi * product.astype(jnp.float32) / period


def row_freqs(height, modes_h):
    index = jnp.arange(modes_h, dtype=jnp.int32)
    return jnp.where(index < modes_h // 2, index, height - modes_h + index).astype(jnp.int32)


def fwd_w_table(cols, modes_w):
    column = jnp.arange(cols, dtype=jnp.int32)
    slot = jnp.arange(2 * modes_w, dtype=jnp.int32)
    angle = turn_table(column, slot // 2, cols)
    return jnp.where(slot[None, :] % 2 == 0, jnp.cos(angle), -jnp.sin(angle)).astype(jnp.bfloat16)


def fwd_h_table(height, modes_h):
    angle = turn_table(jnp.arange(height, dtype=jnp.int32), row_freqs(height, modes_h), height)
    return jnp.concatenate([jnp.cos(angle), jnp.sin(angle)], axis=1).astype(jnp.bfloat16)


def inv_h_table(height, modes_h):
    angle = turn_table(row_freqs(height, modes_h), jnp.arange(height, dtype=jnp.int32), height)
    cosine = jnp.cos(angle) / height
    sine = jnp.sin(angle) / height
    upper = jnp.concatenate([cosine, sine], axis=1)
    lower = jnp.concatenate([-sine, cosine], axis=1)
    return jnp.concatenate([upper, lower], axis=0).astype(jnp.bfloat16)


def inv_w_table(cols, modes_w):
    slot = jnp.arange(2 * modes_w, dtype=jnp.int32)
    mode = slot // 2
    angle = turn_table(mode, jnp.arange(cols, dtype=jnp.int32), cols)
    factor = jnp.where(mode == 0, 1.0, 2.0).astype(jnp.float32)[:, None] / cols
    return jnp.where(slot[:, None] % 2 == 0, factor * jnp.cos(angle), -factor * jnp.sin(angle)).astype(jnp.bfloat16)


def one_layer(field, weights, gain_w, bias, tables):
    fw_tab, eh_tab, gi_tab, gw_tab = tables
    chans = field.shape[0]
    height = field.shape[1]
    modes_h = eh_tab.shape[1] // 2
    modes_w = fw_tab.shape[1] // 2
    upart = jnp.einsum("chw,wk->khc", field.astype(jnp.float32), fw_tab.astype(jnp.float32)).astype(jnp.bfloat16)
    proj = jnp.einsum("khc,hf->kcf", upart.astype(jnp.float32), eh_tab.astype(jnp.float32))
    proj = proj.reshape(modes_w, 2, chans, 2 * modes_h)
    spec_re = (proj[:, 0, :, :modes_h] + proj[:, 1, :, modes_h:]).astype(jnp.bfloat16)
    spec_im = (proj[:, 1, :, :modes_h] - proj[:, 0, :, modes_h:]).astype(jnp.bfloat16)
    wfloat = weights.astype(jnp.float32)
    mixed_re = jnp.einsum("jcf,jfco->jfo", spec_re.astype(jnp.float32), wfloat)
    mixed_im = jnp.einsum("jcf,jfco->jfo", spec_im.astype(jnp.float32), wfloat)
    out_re = (mixed_re[..., :chans] - mixed_im[..., chans:]).astype(jnp.bfloat16)
    out_im = (mixed_re[..., chans:] + mixed_im[..., :chans]).astype(jnp.bfloat16)
    stacked = jnp.stack([out_re, out_im], axis=1).reshape(modes_w, 2 * modes_h, chans)
    zpart = jnp.einsum("jmc,mn->jnc", stacked.astype(jnp.float32), gi_tab.astype(jnp.float32))
    zpart = zpart.reshape(2 * modes_w, height, chans).astype(jnp.bfloat16)
    spec = jnp.einsum("khc,kw->chw", zpart.astype(jnp.float32), gw_tab.astype(jnp.float32))
    point = jnp.einsum("chw,co->ohw", field.astype(jnp.float32), gain_w.astype(jnp.float32))
    point = point + bias.astype(jnp.float32)[:, None, None]
    return jax.nn.gelu(spec + point, approximate=True).astype(jnp.bfloat16)


def reference(features, lift_w, spec_w, point_w, point_b):
    tables = (fwd_w_table(COLS, MODES_W), fwd_h_table(ROWS, MODES_H), inv_h_table(ROWS, MODES_H), inv_w_table(COLS, MODES_W))
    results = []
    for micro_pos in range(MICRO):
        field = jnp.einsum("fhw,fc->chw", features[micro_pos].astype(jnp.float32), lift_w.astype(jnp.float32)).astype(jnp.bfloat16)
        layer_outs = []
        for layer_pos in range(LAYERS):
            field = one_layer(field, spec_w[layer_pos], point_w[layer_pos], point_b[layer_pos], tables)
            layer_outs.append(field)
        results.append(jnp.stack(layer_outs, axis=0))
    return jnp.stack(results, axis=1)
```

```python
import functools

import jax
import jax.numpy as jnp
import numpy as np
from jax import lax
from jax.experimental import pallas as pl
from jax.experimental.pallas import tpu as pltpu
from jax.sharding import PartitionSpec as P

MESH = pl.DeviceIdType.MESH
F32 = jnp.float32
BF16 = jnp.bfloat16

CH = 32
ROWS = 256
COLS = 1024
MW = 64
MH = 128
NSP = 16
NSEC = 8
LR = ROWS // NSP
LM = MW // NSP
W_ROWS = 4096 + 64


def make_tables():
    def tab(a, b, n, fn):
        return fn(2.0 * np.pi * ((a * b) % n) / n)

    bf = lambda x: np.asarray(x, np.float32).astype(BF16)
    freqs = np.where(np.arange(MH) < MH // 2, np.arange(MH), ROWS - MH + np.arange(MH))
    w = np.arange(COLS)
    q, part, j = np.meshgrid(np.arange(NSP), np.arange(2), np.arange(LM), indexing="ij")
    mode = (4 * q + j).reshape(-1)
    part = part.reshape(-1)
    cos = tab(mode[:, None], w[None], COLS, np.cos)
    sin = tab(mode[:, None], w[None], COLS, np.sin)
    fwt = bf(np.where(part[:, None] == 0, cos, -sin))
    s, ib, po, i8 = np.meshgrid(np.arange(2), np.arange(16), np.arange(2), np.arange(8), indexing="ij")
    s, po = s.reshape(-1), po.reshape(-1)
    f = freqs[(ib * 8 + i8).reshape(-1)]
    pt, hh, pp = np.meshgrid(np.arange(2), np.arange(LR), np.arange(NSP), indexing="ij")
    pt = pt.reshape(-1)
    h = (16 * pp + hh).reshape(-1)
    cos = tab(f[:, None], h[None], ROWS, np.cos)
    sin = tab(f[:, None], h[None], ROWS, np.sin)
    xr = np.where(pt[None] == 0, cos, sin)
    xi = np.where(pt[None] == 0, -sin, cos)
    sel = (s * 2 + po)[:, None]
    e2 = bf(np.select([sel == 0, sel == 1, sel == 2, sel == 3], [xr, xi, -xi, xr]))
    p_, hg, h4, q2 = np.meshgrid(np.arange(16), np.arange(4), np.arange(4), np.arange(2), indexing="ij")
    h = (16 * p_ + 4 * hg + h4).reshape(-1)
    q2 = q2.reshape(-1)
    ib, pi_, i8 = np.meshgrid(np.arange(16), np.arange(2), np.arange(8), indexing="ij")
    f = freqs[(ib * 8 + i8).reshape(-1)]
    pi_ = pi_.reshape(-1)
    cos = tab(h[:, None], f[None], ROWS, np.cos) / ROWS
    sin = tab(h[:, None], f[None], ROWS, np.sin) / ROWS
    sel = (pi_[None] * 2 + q2[:, None])
    gi = bf(np.select([sel == 0, sel == 1, sel == 2, sel == 3], [cos, sin, -sin, cos]))
    j, q, h4, q2 = np.meshgrid(np.arange(4), np.arange(16), np.arange(4), np.arange(2), indexing="ij")
    mode = (4 * q + j).reshape(-1)
    q2 = q2.reshape(-1)
    c = np.where(mode == 0, 1.0, 2.0)[:, None] / COLS
    gw = bf(np.where(q2[:, None] == 0, c * tab(mode[:, None], w[None], COLS, np.cos),
                     -c * tab(mode[:, None], w[None], COLS, np.sin)))
    perm = np.zeros((128, 128), np.float32)
    for k in range(8):
        for p in range(16):
            perm[k * 16 + p, p * 8 + k] = 1.0
    rep = np.zeros((128, 512), np.float32)
    for jj in range(4):
        for r in range(4):
            for cc in range(32):
                rep[jj * 32 + cc, jj * 128 + r * 32 + cc] = 1.0
    return fwt, e2, gi, gw, bf(perm), bf(rep)


def roll(x, amount):
    return x if amount % 128 == 0 else pltpu.roll(x, amount % 128, 1)


def chunk_of(shape):
    return lax.broadcasted_iota(jnp.int32, shape, 1) // 32


def by_chunk(parts):
    lane = chunk_of(parts[0].shape)
    out = parts[3]
    for j in (2, 1, 0):
        out = jnp.where(lane == j, parts[j], out)
    return out


def forward_w(fwt, field):
    return lax.dot_general(fwt, field, (((1,), (1,)), ((), ())), preferred_element_type=F32)


def gather_rows(perm, slabs, put):
    v = jnp.dot(perm, slabs, preferred_element_type=F32)
    for part in range(2):
        for hg in range(4):
            src = [
                v[(part * 4 + j) * 16 : (part * 4 + j + 1) * 16, hg * 128 : (hg + 1) * 128]
                for j in range(4)
            ]
            for g in range(4):
                row = (part * 16 + hg * 4 + g) * 16
                put(row, by_chunk([roll(src[j], 32 * (j - g)) for j in range(4)]).astype(BF16))


def spread(e2, rep, spectra):
    x = jnp.dot(e2, spectra, preferred_element_type=F32).astype(BF16)
    return jnp.dot(x, rep, preferred_element_type=F32).astype(BF16)


def mix_pair(get, weights):
    shape = (16, 128)
    row = lax.broadcasted_iota(jnp.int32, shape, 0) % 8
    lane = chunk_of(shape)
    zero = jnp.zeros(shape, BF16)
    rows = []
    for b in range(2):
        for j in range(4):
            blocks = []
            for s in range(2):
                x = get(s, b, j)
                for half in range(2):
                    blocks.append(jnp.where(row == lane + 4 * half, x, zero))
            rows.append(jnp.concatenate(blocks, axis=1))
    lhs = jnp.concatenate(rows, axis=0)
    out = jnp.dot(lhs, weights, preferred_element_type=F32)
    res = []
    for b in range(2):
        res.append(by_chunk([
            out[(b * 4 + j) * 16 : (b * 4 + j + 1) * 16, b * 128 : (b + 1) * 128] for j in range(4)
        ]))
    return jnp.concatenate(res, axis=0).astype(BF16)


def spread_rows(slabs, hg, put):
    t = slabs.T.astype(BF16)
    shape = (32, 128)
    lane = (lax.broadcasted_iota(jnp.int32, shape, 1) // 2) % 4
    zero = jnp.zeros(shape, BF16)
    for h4 in range(4):
        for j in range(4):
            put((hg * 4 + h4) * 32, j * 128, jnp.where(lane == h4, t[j * 32 : (j + 1) * 32], zero))


def gelu(x):
    inner = x * (0.7978845608028654 + 0.035677408136300125 * (x * x))
    half = 0.5 * x
    return half + half * jnp.tanh(inner)


def fused(feat, lift, w_all, fwt, e2, gi, gw, perm, rep, out, *scratch):
    (fields, wts, us, ur, zs, zr, rhs, xrep, y_s, lhs, kron,
     w_sem, u_ssem, u_rsem, z_ssem, z_rsem, o_ssem, o_rsem, o_lsem) = scratch
    sec = lax.axis_index("section")
    me = lax.axis_index("space")

    barrier = pltpu.get_barrier_semaphore()

    def greet_space(d, _):
        pl.semaphore_signal(barrier, inc=1, device_id={"section": sec, "space": lax.rem(me + d, NSP)}, device_id_type=MESH)
        return 0

    def greet_section(d, _):
        pl.semaphore_signal(barrier, inc=1, device_id={"section": lax.rem(sec + d, NSEC), "space": me}, device_id_type=MESH)
        return 0

    lax.fori_loop(1, NSP, greet_space, 0)
    lax.fori_loop(1, NSEC, greet_section, 0)

    def w_copy(l):
        return pltpu.make_async_copy(w_all.at[l], wts.at[l], w_sem.at[l])

    def start_w(l, _):
        w_copy(l).start()
        return 0

    lax.fori_loop(0, NSEC, start_w, 0)

    for r in range(4):
        fields[0, r * 128 : (r + 1) * 128, :] = jnp.dot(
            lift[r * 128 : (r + 1) * 128, :], feat[sec], preferred_element_type=F32
        ).astype(BF16)

    pl.semaphore_wait(barrier, NSP - 1 + NSEC - 1)

    def u_copy(l, peer):
        return pltpu.make_async_remote_copy(
            src_ref=us.at[l, peer], dst_ref=ur.at[l, me], send_sem=u_ssem.at[l], recv_sem=u_rsem.at[l],
            device_id={"section": sec, "space": peer}, device_id_type=MESH)

    def z_copy(l, peer):
        return pltpu.make_async_remote_copy(
            src_ref=zs.at[l, peer], dst_ref=zr.at[l, :, me], send_sem=z_ssem.at[l], recv_sem=z_rsem.at[l],
            device_id={"section": sec, "space": peer}, device_id_type=MESH)

    def u_all(l):
        return pltpu.make_async_remote_copy(
            src_ref=us.at[l, pl.ds(0, NSP - 1)], dst_ref=ur.at[l, pl.ds(0, NSP - 1)],
            send_sem=u_ssem.at[l], recv_sem=u_rsem.at[l],
            device_id={"section": sec, "space": lax.rem(me + 1, NSP)}, device_id_type=MESH)

    def z_all(l):
        return pltpu.make_async_remote_copy(
            src_ref=zs.at[l, pl.ds(0, NSP - 1)], dst_ref=zs.at[l, pl.ds(0, NSP - 1)],
            send_sem=z_ssem.at[l], recv_sem=z_rsem.at[l],
            device_id={"section": sec, "space": lax.rem(me + 1, NSP)}, device_id_type=MESH)

    def out_remote(l):
        return pltpu.make_async_remote_copy(
            src_ref=fields.at[l + 1], dst_ref=out.at[sec], send_sem=o_ssem.at[l], recv_sem=o_rsem.at[sec],
            device_id={"section": l, "space": me}, device_id_type=MESH)

    def out_local(l):
        return pltpu.make_async_copy(fields.at[l + 1], out.at[sec], o_lsem)

    def layer(l, _):
        u = forward_w(fwt[...], fields[l])
        us[l] = u.reshape(NSP, 8, 512).astype(BF16)

        def send_u(d, _):
            u_copy(l, lax.rem(me + d, NSP)).start()
            return 0

        lax.fori_loop(1, NSP, send_u, 0)
        ur[l, me] = us[l, me]
        u_all(l).wait_recv()

        def put_rhs(row, value):
            rhs[row : row + 16, :] = value

        gather_rows(perm[...], ur[l].reshape(128, 512), put_rhs)
        xrep[...] = spread(e2[...], rep[...], rhs[...])

        w_copy(l).wait()

        for ibp in range(8):
            def get(s, b, j, ibp=ibp):
                row = s * 256 + (2 * ibp + b) * 16
                return xrep[row : row + 16, j * 128 : (j + 1) * 128]

            y_s[ibp * 32 : (ibp + 1) * 32, :] = mix_pair(get, wts[l, ibp * 512 : (ibp + 1) * 512, :])

        z = jnp.dot(gi[...], y_s[...], preferred_element_type=F32)
        zs[l] = z.reshape(NSP, 4, 8, 128).astype(BF16)

        def send_z(d, _):
            z_copy(l, lax.rem(me + d, NSP)).start()
            return 0

        lax.fori_loop(1, NSP, send_z, 0)
        zr[l, :, me] = zs[l, me]

        wt = wts[l, 4096:4128, :]
        lane = chunk_of((32, 256))
        for h in range(8):
            kron[h * 32 : (h + 1) * 32, :] = jnp.where(lane == h, wt, jnp.zeros_like(wt))

        z_all(l).wait_recv()

        def put_lhs(row, col, value):
            lhs[row : row + 32, col : col + 128] = value

        for hg in range(4):
            spread_rows(zr[l, hg].astype(F32).reshape(128, 128), hg, put_lhs)

        bias = wts[l, 4128:4160, :].astype(F32)

        def tail(wc, _):
            cols = pl.ds(pl.multiple_of(wc * 256, 256), 256)
            spec = jnp.dot(lhs[...], gw[:, cols], preferred_element_type=F32)
            for rb in range(2):
                rows = slice(rb * 256, (rb + 1) * 256)
                x = spec[rows] + jnp.dot(kron[...], fields[l, rows, cols], preferred_element_type=F32)
                x = (x.reshape(8, 32, 256) + bias[None]).reshape(256, 256)
                fields[l + 1, rows, cols] = gelu(x).astype(BF16)
            return 0

        lax.fori_loop(0, 4, tail, 0)

        @pl.when(l == sec)
        def _():
            out_local(l).start()

        @pl.when(l != sec)
        def _():
            out_remote(l).start()

        return 0

    lax.fori_loop(0, NSEC, layer, 0)

    def finish(l, _):
        u_all(l).wait_send()
        z_all(l).wait_send()

        @pl.when(l == sec)
        def _():
            out_local(l).wait()

        @pl.when(l != sec)
        def _():
            out_remote(l).wait_send()
            pltpu.make_async_remote_copy(
                src_ref=fields.at[0], dst_ref=out.at[l], send_sem=o_ssem.at[l], recv_sem=o_rsem.at[l],
                device_id={"section": l, "space": me}, device_id_type=MESH).wait_recv()

        return 0

    lax.fori_loop(0, NSEC, finish, 0)


def pack_weights(spec_w, point_w, point_b):
    s = spec_w.reshape(LM, 8, 2, 8, CH, 2, CH)
    s = s.transpose(1, 5, 3, 4, 2, 0, 6).reshape(4096, 256)
    wt = jnp.tile(point_w.T, (1, 8))
    bias = jnp.broadcast_to(point_b[:, None], (CH, 256))
    return jnp.concatenate([s, wt, bias], axis=0)


def on_device(features, lift_w, spec_w, point_w, point_b):
    fwt, e2, gi, gw, perm, rep = make_tables()
    feat = features.reshape(NSEC, 2 * LR, COLS)
    eye = jnp.eye(LR, dtype=BF16)
    lift = (lift_w.T[None, :, :, None] * eye[:, None, None, :]).reshape(LR * CH, 2 * LR)
    own = pack_weights(spec_w[0], point_w[0], point_b[0])
    w_all = lax.all_gather(own, "section")
    vmem = pl.BlockSpec(memory_space=pltpu.VMEM)
    hbm = pl.BlockSpec(memory_space=pl.ANY)
    out = pl.pallas_call(
        fused,
        out_shape=jax.ShapeDtypeStruct((NSEC, LR * CH, COLS), BF16),
        in_specs=[vmem, vmem, hbm] + [vmem] * 6,
        out_specs=hbm,
        scratch_shapes=[
            pltpu.VMEM((NSEC + 1, LR * CH, COLS), BF16),
            pltpu.VMEM((NSEC, W_ROWS, 256), BF16),
            pltpu.VMEM((NSEC, NSP, 8, 512), BF16),
            pltpu.VMEM((NSEC, NSP, 8, 512), BF16),
            pltpu.VMEM((NSEC, NSP, 4, 8, 128), BF16),
            pltpu.VMEM((NSEC, 4, NSP, 8, 128), BF16),
            pltpu.VMEM((512, 128), BF16),
            pltpu.VMEM((512, 512), BF16),
            pltpu.VMEM((256, 128), BF16),
            pltpu.VMEM((512, 512), BF16),
            pltpu.VMEM((256, 256), BF16),
            pltpu.SemaphoreType.DMA((NSEC,)),
            pltpu.SemaphoreType.DMA((NSEC,)),
            pltpu.SemaphoreType.DMA((NSEC,)),
            pltpu.SemaphoreType.DMA((NSEC,)),
            pltpu.SemaphoreType.DMA((NSEC,)),
            pltpu.SemaphoreType.DMA((NSEC,)),
            pltpu.SemaphoreType.DMA((NSEC,)),
            pltpu.SemaphoreType.DMA,
        ],
        compiler_params=pltpu.CompilerParams(
            collective_id=0, has_side_effects=True, vmem_limit_bytes=60 << 20
        ),
        name="fused",
    )(feat, lift, w_all, fwt, e2, gi, gw, perm, rep)
    out = out.reshape(NSEC, LR, CH, COLS).transpose(0, 2, 1, 3)
    return out[None]


def solution(mesh):
    in_specs = (
        P(None, None, "space", None),
        P(),
        P("section", "space", None, None, None),
        P("section", None, None),
        P("section", None),
    )
    out_specs = P("section", None, None, "space", None)
    return jax.shard_map(
        on_device, mesh=mesh, in_specs=in_specs, out_specs=out_specs, check_vma=False
    )
```
